32 devices in a mesh: rep: 2 (over x), pts: 16 (over z, y, core).
Axes of the slice: x: 2, y: 2, z: 4, core: 2. Of those that a mesh axis runs over, the one named last changes fastest.
Arguments:
- orbitals: bfloat16 [64, 32, 512], P(('rep', 'pts')), parts along dimension 0, may hold values from -6 to 6
- points: bfloat16 [12288, 512], P('pts'), may hold values from -0.25 to 0.25
- coupling: bfloat16 [12288, 4096], P('pts'), may hold values from -0.01953125 to 0.01953125
- fields: int32 [64, 4096], P('rep'), parts along dimension 0, may hold values from 0 to 3
- destination: int32 [64], P('rep'), parts along dimension 0, may hold values from 0 to 15, as said below
Outputs:
- moved: bfloat16 [96, 32, 512], P(('rep', 'pts')), parts along dimension 0
The draws below stay inside these ranges and needn't reach their ends.
There are 2 independent parts, one for each index of `rep`. The reference program is written for one: setup_inputs(seed, part) draws one part's arguments, and reference() takes and returns one part's arrays. A program takes and returns all parts, laid end to end along the dimension named above; an argument that names none is the same for every part. Nothing has to cross between parts.
Inputs may be any that keep to these rules, and one draw needn't show every extreme that they name: Each group is the destination of at most 3 walkers; some group receives exactly 3, and the 2 walkers of some group all go to it.
All inputs are finite; a program needn't handle non-finite values.
Results may differ from the reference program's by a relative error of at most 0.008.
Values may be sent and summed in bfloat16 or wider, within the bound.
A program may use at most 64 MiB of HBM per device.

```python
import jax
import jax.numpy as jnp
from jax import lax

N_ORB = 512
NOCC = 16
NPTS = 12288
NFIELD = 4096
W_DEV = 2
CAP = 3
WALKERS = 32
N_PTS = 16


def draw_destination(key, part):
    slots_all = N_PTS * CAP
    count_all = W_DEV * N_PTS
    group_key = jax.random.fold_in(key, 11)
    noise_key = jax.random.fold_in(key, 12)
    offset_key = jax.random.fold_in(key, 13)
    chosen_group = jax.random.randint(group_key, (), 0, N_PTS)
    noise = jax.random.randint(noise_key, (slots_all,), 0, 1 << 16)
    slot_ids = jnp.arange(slots_all, dtype=jnp.int32)
    scores = noise * slots_all + slot_ids
    scores = jnp.where(slot_ids // CAP == chosen_group, slot_ids - slots_all, scores)
    ordering = jnp.argsort(scores, stable=True).astype(jnp.int32)
    picked = ordering[:count_all] // CAP
    offset = jax.random.randint(offset_key, (), 0, N_PTS) * W_DEV
    return jnp.roll(picked, offset).astype(jnp.int32)


def place_ends(drawn, own_key, least, largest):
    longest = drawn.shape.index(max(drawn.shape))
    spots = []
    for shift in (0, 1):
        where = [jax.random.randint(jax.random.fold_in(own_key, axis), (), 0, length) for axis, length in enumerate(drawn.shape)]
        where[longest] = (where[longest] + shift) % drawn.shape[longest]
        spots.append(tuple(where))
    return drawn.at[spots[0]].set(least).at[spots[1]].set(largest)


def steps_of(own_key, extent, split, least, high):
    gain, own = 1.0, jax.random.fold_in(own_key, 6)
    for position, parts in split:
        heights = jnp.exp(jax.random.uniform(jax.random.fold_in(own, position), (parts,), jnp.float32, least / len(split), high / len(split)))
        gain = gain * jnp.repeat(heights, extent[position] // parts).reshape([-1 if axis == position else 1 for axis in range(len(extent))])
    return gain


def centred(stream_key, extent, spread, most, shards=(), kind=jnp.bfloat16):
    array = jax.random.normal(stream_key, extent, jnp.float32) * spread
    if len(shards) > 0:
        array = steps_of(stream_key, extent, shards, -0.22, 0.18) * array
    return jnp.clip(array, min=-most, max=most).astype(kind)


def setup_inputs(seed: int = 0, part: int = 0) -> dict:
    streams_of = jax.random.split(jax.random.key(seed), 6)
    part_keys = jax.random.split(jax.random.fold_in(streams_of[5], part), 6)
    orbitals = centred(part_keys[0], (WALKERS, 2 * NOCC, N_ORB), 1.0, 6.0, ((0, 16),))
    points = centred(streams_of[1], (NPTS, N_ORB), N_ORB ** -0.5, 0.25, ((0, 16),))
    coupling = centred(streams_of[2], (NPTS, NFIELD), (0.09 * NFIELD ** -0.5), 0.01953125, ((0, 16),))
    fields = place_ends(jax.random.randint(part_keys[3], (WALKERS, NFIELD), 0, 4), jax.random.fold_in(part_keys[3], 1), 0, 3).astype(jnp.int32)
    destination = draw_destination(jax.random.fold_in(jax.random.fold_in(streams_of[5], part), 71), part)
    return {"orbitals": orbitals, "points": points, "coupling": coupling, "fields": fields, "destination": destination}


LEVELS = (-2.3344142183389773, -0.7419637843027258, 0.7419637843027258, 2.3344142183389773)


def field_values(fields):
    values = jnp.zeros(fields.shape, jnp.float32)
    for level_index in range(4):
        values = values + jnp.where(fields == level_index, LEVELS[level_index], 0.0)
    return values.astype(jnp.bfloat16)


def rotate(block):
    half_rows = block.shape[-2] // 2
    return jnp.concatenate([-block[..., half_rows:, :], block[..., :half_rows, :]], axis=-2)


def apply_field(rows, points, scale):
    table = points.astype(jnp.float32)
    inner = jnp.einsum('wrn,pn->wrp', rows.astype(jnp.float32), table)
    scaled = lax.optimization_barrier((inner * scale[:, None, :]).astype(jnp.bfloat16))
    return rotate(jnp.einsum('wrp,pn->wrn', scaled.astype(jnp.float32), table))


def reference(orbitals, points, coupling, fields, destination):
    values = field_values(fields)
    scale = jnp.dot(values, coupling.T, preferred_element_type=jnp.float32)
    first = apply_field(orbitals, points, scale)
    first_rounded = lax.optimization_barrier(first.astype(jnp.bfloat16))
    second = 0.5 * apply_field(first_rounded, points, scale)
    propagated = (orbitals.astype(jnp.float32) + first + second).astype(jnp.bfloat16)
    walker_ids = jnp.arange(destination.shape[0], dtype=jnp.int32)
    earlier = (destination[:, None] == destination[None, :]) & (walker_ids[None, :] < walker_ids[:, None])
    target = destination * CAP + jnp.sum(earlier.astype(jnp.int32), axis=1).astype(jnp.int32)
    moved = jnp.zeros((N_PTS * CAP,) + propagated.shape[1:], jnp.bfloat16)
    return moved.at[target].set(propagated)
```

```python
import jax
import jax.numpy as jnp
from jax import lax
from jax.sharding import PartitionSpec as P

LEVELS = (-2.3344142183389773, -0.7419637843027258, 0.7419637843027258, 2.3344142183389773)


def field_values(fields):
    values = jnp.zeros(fields.shape, jnp.float32)
    for level_index in range(4):
        values = values + jnp.where(fields == level_index, LEVELS[level_index], 0.0)
    return values.astype(jnp.bfloat16)


def rotate(block):
    half_rows = block.shape[-2] // 2
    return jnp.concatenate([-block[..., half_rows:, :], block[..., :half_rows, :]], axis=-2)


def arrival_targets(destination, slot_count):
    walker_ids = jnp.arange(destination.shape[0], dtype=jnp.int32)
    earlier = (destination[:, None] == destination[None, :]) & (
        walker_ids[None, :] < walker_ids[:, None]
    )
    return destination * slot_count + jnp.sum(earlier.astype(jnp.int32), axis=1)


def place_rows(rows_all, targets, position, slot_count):
    flattened = rows_all.reshape(rows_all.shape[0], -1)
    slot_ids = position * slot_count + jnp.arange(slot_count, dtype=jnp.int32)
    selector = (targets[None, :] == slot_ids[:, None]).astype(jnp.bfloat16)
    placed = jnp.dot(selector, flattened, preferred_element_type=jnp.float32).astype(jnp.bfloat16)
    return placed.reshape((slot_count,) + rows_all.shape[1:])


def per_device(orbitals, points, coupling, fields, destination):
    own_count = orbitals.shape[0]
    slot_count = own_count + own_count // 2
    position = lax.axis_index("pts")
    targets = arrival_targets(destination, slot_count)
    values = field_values(fields)
    scale = jnp.einsum("wg,pg->wp", values, coupling, preferred_element_type=jnp.float32)

    def apply(rows):
        gathered = lax.all_gather(rows, "pts", axis=0, tiled=True)
        inner = jnp.einsum("wrn,pn->wrp", gathered, points, preferred_element_type=jnp.float32)
        scaled = (inner * scale[:, None, :]).astype(jnp.bfloat16)
        partial = jnp.einsum("wrp,pn->wrn", scaled, points, preferred_element_type=jnp.float32)
        return rotate(
            lax.psum_scatter(partial.astype(jnp.bfloat16), "pts", scatter_dimension=0, tiled=True).astype(jnp.float32)
        )

    first = apply(orbitals)
    second = 0.5 * apply(first.astype(jnp.bfloat16))
    propagated = (orbitals.astype(jnp.float32) + first + second).astype(jnp.bfloat16)
    everyone = lax.all_gather(propagated, "pts", axis=0, tiled=True)
    return place_rows(everyone, targets, position, slot_count)


def solution(mesh):
    return jax.shard_map(
        per_device,
        mesh=mesh,
        in_specs=(
            P(("rep", "pts"), None, None),
            P("pts", None),
            P("pts", None),
            P("rep", None),
            P("rep"),
        ),
        out_specs=P(("rep", "pts"), None, None),
        check_vma=False,
    )
```

```python
import functools

import jax
import jax.numpy as jnp
from jax import lax
from jax.experimental import pallas as pl
from jax.experimental.pallas import tpu as pltpu
from jax.sharding import PartitionSpec as P

LEVELS = (-2.3344142183389773, -0.7419637843027258, 0.7419637843027258, 2.3344142183389773)
MESH = pl.DeviceIdType.MESH
GROUP = 4
PIECES = 3


def flip(index, bit):
    return index + bit - 2 * bit * (lax.rem(index // bit, 2))


def kernel(
    reps, line, loc_ref, set_ref, orb_hbm, pts_hbm, coup_hbm, fields_hbm, out_ref,
    orb, coup, fields, pts, scale_out, scale, rows, acc, part, part_in, first, first_out, rows2,
    part2, part2_in, prop, props, give, take,
    load_sem, coup_sem, line_send, line_recv, grp_send, grp_recv, pts_send, pts_recv,
):
    own, height, width = orb.shape
    block = own * height
    count = pts.shape[1]
    half = count // 2
    piece = half // PIECES
    slots = out_ref.shape[0]
    rep = lax.axis_index("rep")
    me = lax.axis_index("pts")
    mine = lax.rem(me, GROUP)
    place = me // GROUP
    side = lax.rem(rep, 2)
    other_rep = flip(rep, 1)
    core = flip(me, 1)
    across = flip(me, 2)
    mine_core, mine_across = flip(mine, 1), flip(mine, 2)
    mine_far = flip(mine_across, 1)

    load = [
        pltpu.make_async_copy(fields_hbm, fields, load_sem.at[0]),
        pltpu.make_async_copy(pts_hbm, pts.at[mine], load_sem.at[1]),
        pltpu.make_async_copy(orb_hbm, orb, load_sem.at[2]),
    ]
    for copy in load:
        copy.start()
    tile = coup.shape[1]
    coup_loads = [
        pltpu.make_async_copy(coup_hbm.at[pl.ds(c * tile, tile)], coup.at[c], coup_sem.at[c])
        for c in range(coup.shape[0])
    ]
    for copy in coup_loads:
        copy.start()

    barrier = pltpu.get_barrier_semaphore()
    line_mates = [(lax.rem(place + d, line), lax.rem(place + d, line) * GROUP + mine) for d in range(1, line)]
    group_mates = [(lax.rem(mine + d, GROUP), place * GROUP + lax.rem(mine + d, GROUP)) for d in range(1, GROUP)]
    for _, mate in line_mates + group_mates:
        pl.semaphore_signal(barrier, inc=1, device_id={"rep": rep, "pts": mate}, device_id_type=MESH)
    pl.semaphore_signal(barrier, inc=1, device_id={"rep": other_rep, "pts": me}, device_id_type=MESH)
    pl.semaphore_wait(barrier, len(line_mates) + len(group_mates) + 1)

    def remote(src, dst, send, recv, target, target_rep=None):
        return pltpu.make_async_remote_copy(
            src_ref=src, dst_ref=dst, send_sem=send, recv_sem=recv,
            device_id={"rep": rep if target_rep is None else target_rep, "pts": target},
            device_id_type=MESH,
        )

    def line_copies(phase, source, landing):
        return [
            remote(source(slot), landing.at[place], line_send.at[phase, slot], line_recv.at[phase, place], mate)
            for slot, mate in line_mates
        ]

    def line_arrivals(phase, landing):
        for slot, mate in line_mates:
            remote(landing.at[slot], landing.at[slot], line_send.at[phase, slot], line_recv.at[phase, slot], mate).wait_recv()

    started = []

    def go(copies):
        for copy in copies:
            copy.start()
            started.append(copy)

    def piece_of(which, part_side, number):
        return pts.at[which, pl.ds(pl.multiple_of(part_side * half + number * piece, 16), piece)]

    load[2].wait()
    go(line_copies(0, lambda slot: orb, rows))
    load[1].wait()
    go([
        remote(piece_of(mine, side, n), piece_of(mine, side, n), pts_send.at[0, n], pts_recv.at[0, n], across)
        for n in range(PIECES)
    ])
    go([remote(pts.at[mine], pts.at[mine], pts_send.at[4, 0], pts_recv.at[4, 0], core)])
    rows[place] = orb[...]

    load[0].wait()
    levels = jnp.zeros(fields.shape, jnp.float32)
    for level_index in range(4):
        levels = jnp.where(fields[...] == level_index, LEVELS[level_index], levels)
    values = levels.astype(jnp.bfloat16)
    for c in range(coup.shape[0]):
        coup_loads[c].wait()
        got = lax.dot_general(
            values, coup[c], (((1,), (1,)), ((), ())), preferred_element_type=jnp.float32
        )
        for k in range(line):
            for j in range(GROUP):
                start = (k * GROUP + j) * own
                scale_out[j, pl.ds(k * own, own), pl.ds(c * tile, tile)] = got[start:start + own]
    go([
        remote(scale_out.at[j], scale.at[mine], grp_send.at[0, j], grp_recv.at[0, mine], mate)
        for j, mate in group_mates
    ])
    scale[mine] = scale_out[mine]

    for n in range(PIECES):
        remote(piece_of(mine_across, side, n), piece_of(mine_across, side, n), pts_send.at[0, n], pts_recv.at[0, n], across).wait_recv()
        src = piece_of(mine_across, side, n)
        go([
            remote(src, src, pts_send.at[1, n], pts_recv.at[1, n], me, other_rep),
            remote(src, src, pts_send.at[2, n], pts_recv.at[2, n], core),
        ])

    width_chunk = 256 if count % 256 == 0 else count
    walkers = line * own

    def apply_block(which, rows_ref, fresh):
        def body(c, _):
            at = pl.multiple_of(c * width_chunk, width_chunk)
            table = pts[which, pl.ds(at, width_chunk), :]
            if width_chunk == count:
                weight = scale[which]
            else:
                weight = scale[which, :, pl.ds(at, width_chunk)]
            left = rows_ref[...].reshape(line * block, width)
            inner = lax.dot_general(left, table, (((1,), (1,)), ((), ())), preferred_element_type=jnp.float32)
            scaled = (inner.reshape(walkers, height, width_chunk) * weight[:, None, :]).astype(jnp.bfloat16)
            out = jnp.dot(scaled.reshape(line * block, width_chunk), table, preferred_element_type=jnp.float32)
            acc[...] += out.reshape(acc.shape)
            return 0

        if fresh:
            acc[...] = jnp.zeros_like(acc)
        lax.fori_loop(0, count // width_chunk, body, 0)

    def turn(block_value):
        low = block_value[:, : height // 2]
        high = block_value[:, height // 2:]
        return jnp.concatenate([-high, low], axis=1)

    def scale_arrived(slot):
        remote(scale.at[slot], scale.at[slot], grp_send.at[0, slot], grp_recv.at[0, slot], me - mine + slot).wait_recv()

    line_arrivals(0, rows)
    apply_block(mine, rows, True)
    scale_arrived(mine_core)
    remote(pts.at[mine_core], pts.at[mine_core], pts_send.at[4, 0], pts_recv.at[4, 0], core).wait_recv()
    apply_block(mine_core, rows, False)
    for n in range(PIECES):
        src = piece_of(mine_across, 1 - side, n)
        remote(src, src, pts_send.at[1, n], pts_recv.at[1, n], me, other_rep).wait_recv()
        go([remote(src, src, pts_send.at[3, n], pts_recv.at[3, n], core)])
    scale_arrived(mine_across)
    apply_block(mine_across, rows, False)
    scale_arrived(mine_far)
    for n in range(PIECES):
        src = piece_of(mine_far, side, n)
        remote(src, src, pts_send.at[2, n], pts_recv.at[2, n], core).wait_recv()
        src = piece_of(mine_far, 1 - side, n)
        remote(src, src, pts_send.at[3, n], pts_recv.at[3, n], core).wait_recv()
    apply_block(mine_far, rows, False)

    def collect(landing):
        total = acc[place]
        for slot, _ in line_mates:
            total = total + landing[slot].astype(jnp.float32)
        return turn(total)

    part[...] = acc[...].astype(jnp.bfloat16)
    go(line_copies(1, lambda slot: part.at[slot], part_in))
    line_arrivals(1, part_in)
    first[...] = collect(part_in)
    first_out[...] = first[...].astype(jnp.bfloat16)
    go(line_copies(2, lambda slot: first_out, rows2))
    rows2[place] = first_out[...]
    line_arrivals(2, rows2)

    apply_block(mine, rows2, True)
    apply_block(mine_core, rows2, False)
    apply_block(mine_across, rows2, False)
    apply_block(mine_far, rows2, False)
    part2[...] = acc[...].astype(jnp.bfloat16)
    go(line_copies(3, lambda slot: part2.at[slot], part2_in))
    line_arrivals(3, part2_in)
    second = 0.5 * collect(part2_in)
    prop[...] = (orb[...].astype(jnp.float32) + first[...] + second).astype(jnp.bfloat16)

    go(line_copies(4, lambda slot: prop, props))
    props[place] = prop[...]
    line_arrivals(4, props)

    def pick(j, s):
        where = loc_ref[(place * GROUP + j) * slots + s]
        return props[where // own, lax.rem(where, own)]

    for j, mate in group_mates:
        for s in range(slots):
            give[j, s] = pick(j, s)
    go([
        remote(give.at[j], take.at[mine], grp_send.at[1, j], grp_recv.at[1, mine], mate)
        for j, mate in group_mates
    ])
    for s in range(slots):
        take[mine, s] = pick(mine, s)
    for j, mate in group_mates:
        remote(take.at[j], take.at[j], grp_send.at[1, j], grp_recv.at[1, j], mate).wait_recv()
    for s in range(slots):
        origin = set_ref[me * slots + s]
        found = take[jnp.maximum(origin, 0), s]
        out_ref[s] = jnp.where(origin >= 0, found, jnp.zeros_like(found))
    for copy in started:
        copy.wait_send()


def arrival_targets(destination, slot_count):
    walker_ids = jnp.arange(destination.shape[0], dtype=jnp.int32)
    earlier = (destination[:, None] == destination[None, :]) & (
        walker_ids[None, :] < walker_ids[:, None]
    )
    return destination * slot_count + jnp.sum(earlier.astype(jnp.int32), axis=1)


def per_device(orbitals, points, coupling, fields, destination):
    own, height, width = orbitals.shape
    slots = own + own // 2
    members = lax.axis_size("pts")
    reps = lax.axis_size("rep")
    line = members // GROUP
    count, field_count = coupling.shape
    targets = arrival_targets(destination, slots)
    slot_ids = jnp.arange(members * slots, dtype=jnp.int32)
    walker_ids = jnp.arange(destination.shape[0], dtype=jnp.int32)
    source = jnp.max(jnp.where(targets[None, :] == slot_ids[:, None], walker_ids[None, :], -1), axis=1)
    known = jnp.maximum(source, 0)
    owner = known // own
    location = (owner // GROUP) * own + known % own
    origin = jnp.where(source >= 0, owner % GROUP, -1)
    tile = 128 if count % 128 == 0 else count
    block = (own, height, width)
    low = jnp.bfloat16
    return pl.pallas_call(
        functools.partial(kernel, reps, line),
        out_shape=jax.ShapeDtypeStruct((slots, height, width), low),
        in_specs=[pl.BlockSpec(memory_space=pltpu.SMEM)] * 2 + [pl.BlockSpec(memory_space=pl.ANY)] * 4,
        out_specs=pl.BlockSpec(memory_space=pltpu.VMEM),
        scratch_shapes=[
            pltpu.VMEM(block, low),
            pltpu.VMEM((count // tile, tile, field_count), low),
            pltpu.VMEM(fields.shape, jnp.int32),
            pltpu.VMEM((GROUP, count, width), low),
            pltpu.VMEM((GROUP, line * own, count), jnp.float32),
            pltpu.VMEM((GROUP, line * own, count), jnp.float32),
            pltpu.VMEM((line,) + block, low),
            pltpu.VMEM((line,) + block, jnp.float32),
            pltpu.VMEM((line,) + block, low),
            pltpu.VMEM((line,) + block, low),
            pltpu.VMEM(block, jnp.float32),
            pltpu.VMEM(block, low),
            pltpu.VMEM((line,) + block, low),
            pltpu.VMEM((line,) + block, low),
            pltpu.VMEM((line,) + block, low),
            pltpu.VMEM(block, low),
            pltpu.VMEM((line,) + block, low),
            pltpu.VMEM((GROUP, slots, height, width), low),
            pltpu.VMEM((GROUP, slots, height, width), low),
            pltpu.SemaphoreType.DMA((3,)),
            pltpu.SemaphoreType.DMA((count // tile,)),
            pltpu.SemaphoreType.DMA((5, line)),
            pltpu.SemaphoreType.DMA((5, line)),
            pltpu.SemaphoreType.DMA((2, GROUP)),
            pltpu.SemaphoreType.DMA((2, GROUP)),
            pltpu.SemaphoreType.DMA((5, PIECES)),
            pltpu.SemaphoreType.DMA((5, PIECES)),
        ],
        compiler_params=pltpu.CompilerParams(collective_id=0, has_side_effects=True, vmem_limit_bytes=60000 * 1024),
    )(location, origin, orbitals, points, coupling, fields)


def solution(mesh):
    return jax.shard_map(
        per_device,
        mesh=mesh,
        in_specs=(
            P(("rep", "pts"), None, None),
            P("pts", None),
            P("pts", None),
            P("rep", None),
            P("rep"),
        ),
        out_specs=P(("rep", "pts"), None, None),
        check_vma=False,
    )
```

```python
import functools

import jax
import jax.numpy as jnp
from jax import lax
from jax.experimental import pallas as pl
from jax.experimental.pallas import tpu as pltpu
from jax.sharding import PartitionSpec as P

LEVELS = (-2.3344142183389773, -0.7419637843027258, 0.7419637843027258, 2.3344142183389773)
MESH = pl.DeviceIdType.MESH
GROUP = 4
PIECES = 3


def flip(index, bit):
    return index + bit - 2 * bit * (lax.rem(index // bit, 2))


def kernel(
    line, loc_ref, set_ref, orb_hbm, pts_hbm, coup_hbm, fields_hbm, out_ref,
    orb, coup, fields, pts, scale_out, scale, rows, acc, part, part_in, first, first_out, rows2,
    part2, part2_in, prop, props, give, take,
    load_sem, coup_sem, line_send, line_recv, grp_send, grp_recv, pts_send, pts_recv,
):
    own, height, width = orb.shape
    half = pts.shape[2]
    piece = half // PIECES
    slots = out_ref.shape[0]
    walkers = line * own
    rep = lax.axis_index("rep")
    me = lax.axis_index("pts")
    mine = lax.rem(me, GROUP)
    place = me // GROUP
    side = lax.rem(rep, 2)
    other_rep = flip(rep, 1)
    core = flip(me, 1)
    across = flip(me, 2)
    mine_core, mine_across = flip(mine, 1), flip(mine, 2)
    mine_far = flip(mine_across, 1)

    load = [
        pltpu.make_async_copy(fields_hbm, fields, load_sem.at[0]),
        pltpu.make_async_copy(pts_hbm, pts.at[mine], load_sem.at[1]),
        pltpu.make_async_copy(orb_hbm, orb, load_sem.at[2]),
    ]
    for n in (1, 2, 0):
        load[n].start()
    tile = coup.shape[1]
    coup_loads = [
        pltpu.make_async_copy(coup_hbm.at[pl.ds(c * tile, tile)], coup.at[c], coup_sem.at[c])
        for c in range(coup.shape[0])
    ]
    for copy in coup_loads:
        copy.start()

    barrier = pltpu.get_barrier_semaphore()

    line_mates = [(lax.rem(place + d, line), lax.rem(place + d, line) * GROUP + mine) for d in range(1, line)]
    group_slots = [lax.rem(mine + d, GROUP) for d in range(1, GROUP)]
    group_mates = [(slot, place * GROUP + slot) for slot in group_slots]
    for _, mate in line_mates + group_mates:
        pl.semaphore_signal(barrier, inc=1, device_id={"rep": rep, "pts": mate}, device_id_type=MESH)
    pl.semaphore_signal(barrier, inc=1, device_id={"rep": other_rep, "pts": me}, device_id_type=MESH)
    pl.semaphore_wait(barrier, len(line_mates) + len(group_mates) + 1)

    def remote(src, dst, send, recv, target, target_rep=None):
        return pltpu.make_async_remote_copy(
            src_ref=src, dst_ref=dst, send_sem=send, recv_sem=recv,
            device_id={"rep": rep if target_rep is None else target_rep, "pts": target},
            device_id_type=MESH,
        )

    started = []

    def go(copies):
        for copy in copies:
            copy.start()
            started.append(copy)

    def line_go(phase, h, source, landing):
        go([
            remote(source(slot), landing(place), line_send.at[phase, h, slot], line_recv.at[phase, h, place], mate)
            for slot, mate in line_mates
        ])

    def line_arrivals(phase, h, landing):
        for slot, mate in line_mates:
            remote(
                landing(slot), landing(slot), line_send.at[phase, h, slot], line_recv.at[phase, h, slot], mate
            ).wait_recv()

    def piece_of(which, part_side, number):
        return pts.at[which, part_side, pl.ds(number * piece, piece)]

    def piece_copy(stage, which, part_side, n, target, target_rep=None):
        src = piece_of(which, part_side, n)
        return remote(src, src, pts_send.at[stage, n], pts_recv.at[stage, n], target, target_rep)

    load[1].wait()
    go([piece_copy(0, mine, side, n, across) for n in range(PIECES)])
    load[2].wait()
    for h in range(own):
        line_go(0, h, lambda slot: orb.at[h], lambda slot: rows[h].at[slot])
    go([remote(pts.at[mine], pts.at[mine], pts_send.at[4, 0], pts_recv.at[4, 0], core)])
    for h in range(own):
        rows[h][place] = orb[h]

    load[0].wait()
    levels = jnp.zeros(fields.shape, jnp.float32)
    for level_index in range(4):
        levels = jnp.where(fields[...] == level_index, LEVELS[level_index], levels)
    values = levels.astype(jnp.bfloat16)
    per_half = half // tile
    for c in range(coup.shape[0]):
        coup_loads[c].wait()
        got = lax.dot_general(
            values, coup[c], (((1,), (1,)), ((), ())), preferred_element_type=jnp.float32
        )
        columns = pl.ds((c % per_half) * tile, tile)
        for k in range(line):
            for j in range(GROUP):
                for h in range(own):
                    w = (k * GROUP + j) * own + h
                    scale_out[j, c // per_half, pl.ds(h * line + k, 1), columns] = got[w:w + 1]
    go([
        remote(scale_out.at[j], scale.at[mine], grp_send.at[0, j], grp_recv.at[0, mine], mate)
        for j, mate in group_mates
    ])
    scale[mine] = scale_out[mine]

    def apply_half(which, part_side, left, at, size):
        table = pts[which, part_side]
        weight = scale[which, part_side][at:at + size]
        flat = left.reshape(size * height, width)
        inner = lax.dot_general(flat, table, (((1,), (1,)), ((), ())), preferred_element_type=jnp.float32)
        scaled = (inner.reshape(size, height, half) * weight[:, None, :]).astype(jnp.bfloat16)
        out = jnp.dot(scaled.reshape(size * height, half), table, preferred_element_type=jnp.float32)
        return out

    def first_half(which, part_side):
        left = jnp.concatenate([r[...] for r in rows], axis=0)
        out = apply_half(which, part_side, left, 0, walkers)
        acc[...] += out.reshape(acc.shape)

    def turn(block_value):
        low = block_value[: height // 2]
        high = block_value[height // 2:]
        return jnp.concatenate([-high, low], axis=0)

    def scale_arrived(slot):
        remote(scale.at[slot], scale.at[slot], grp_send.at[0, slot], grp_recv.at[0, slot], me - mine + slot).wait_recv()

    def from_across(n):
        piece_copy(0, mine_across, side, n, across).wait_recv()
        go([
            piece_copy(1, mine_across, side, n, me, other_rep),
            piece_copy(2, mine_across, side, n, core),
        ])

    def from_rep(n):
        piece_copy(1, mine_across, 1 - side, n, me, other_rep).wait_recv()
        go([piece_copy(3, mine_across, 1 - side, n, core)])

    for n in range(PIECES):
        from_across(n)
    acc[...] = jnp.zeros_like(acc)
    for h in range(own):
        line_arrivals(0, h, lambda slot: rows[h].at[slot])

    def pair(which):
        for part_side in range(2):
            first_half(which, part_side)

    pair(mine)
    for slot in group_slots:
        scale_arrived(slot)
    remote(pts.at[mine_core], pts.at[mine_core], pts_send.at[4, 0], pts_recv.at[4, 0], core).wait_recv()
    pair(mine_core)
    for n in range(PIECES):
        from_rep(n)
    pair(mine_across)
    for n in range(PIECES):
        piece_copy(2, mine_far, side, n, core).wait_recv()
        piece_copy(3, mine_far, 1 - side, n, core).wait_recv()
    pair(mine_far)

    def collect(h, landing):
        total = acc[h, place]
        for slot, _ in line_mates:
            total = total + landing[h][slot].astype(jnp.float32)
        return turn(total)

    for h in range(own):
        part[h][...] = acc[h].astype(jnp.bfloat16)
        line_go(1, h, lambda slot: part[h].at[slot], lambda slot: part_in[h].at[slot])
    for h in range(own):
        line_arrivals(1, h, lambda slot: part_in[h].at[slot])
        first[h] = collect(h, part_in)
        first_out[h][...] = first[h].astype(jnp.bfloat16)
        line_go(2, h, lambda slot: first_out[h], lambda slot: rows2[h].at[slot])
        rows2[h][place] = first_out[h][...]

    for h in range(own):
        line_arrivals(2, h, lambda slot: rows2[h].at[slot])
        acc[h] = jnp.zeros_like(acc[h])

        def second_half(i, _):
            out = apply_half(i // 2, lax.rem(i, 2), rows2[h][...], h * line, line)
            acc[h] += out.reshape(line, height, width)
            return 0

        lax.fori_loop(0, 2 * GROUP, second_half, 0)
        part2[h][...] = acc[h].astype(jnp.bfloat16)
        line_go(3, h, lambda slot: part2[h].at[slot], lambda slot: part2_in[h].at[slot])
    for h in range(own):
        line_arrivals(3, h, lambda slot: part2_in[h].at[slot])
        second = 0.5 * collect(h, part2_in)
        prop[h][...] = (orb[h].astype(jnp.float32) + first[h] + second).astype(jnp.bfloat16)
        line_go(4, h, lambda slot: prop[h], lambda slot: props[h].at[slot])
        props[h][place] = prop[h][...]

    for h in range(own):
        line_arrivals(4, h, lambda slot: props[h].at[slot])

    def pick(j, s):
        where = loc_ref[(place * GROUP + j) * slots + s]
        at = where // own
        picked = props[0][at]
        for h in range(1, own):
            picked = jnp.where(lax.rem(where, own) == h, props[h][at], picked)
        return picked

    for j, mate in group_mates:
        for s in range(slots):
            give[j, s] = pick(j, s)
    go([
        remote(give.at[j], take.at[mine], grp_send.at[1, j], grp_recv.at[1, mine], mate)
        for j, mate in group_mates
    ])
    for s in range(slots):
        take[mine, s] = pick(mine, s)
    for j, mate in group_mates:
        remote(take.at[j], take.at[j], grp_send.at[1, j], grp_recv.at[1, j], mate).wait_recv()
    for s in range(slots):
        origin = set_ref[me * slots + s]
        found = take[jnp.maximum(origin, 0), s]
        out_ref[s] = jnp.where(origin >= 0, found, jnp.zeros_like(found))
    for copy in started:
        copy.wait_send()


def arrival_targets(destination, slot_count):
    walker_ids = jnp.arange(destination.shape[0], dtype=jnp.int32)
    earlier = (destination[:, None] == destination[None, :]) & (
        walker_ids[None, :] < walker_ids[:, None]
    )
    return destination * slot_count + jnp.sum(earlier.astype(jnp.int32), axis=1)


def per_device(orbitals, points, coupling, fields, destination):
    own, height, width = orbitals.shape
    slots = own + own // 2
    line = lax.axis_size("pts") // GROUP
    count, field_count = coupling.shape
    members = lax.axis_size("pts")
    targets = arrival_targets(destination, slots)
    slot_ids = jnp.arange(members * slots, dtype=jnp.int32)
    walker_ids = jnp.arange(destination.shape[0], dtype=jnp.int32)
    source = jnp.max(jnp.where(targets[None, :] == slot_ids[:, None], walker_ids[None, :], -1), axis=1)
    known = jnp.maximum(source, 0)
    owner = known // own
    location = (owner // GROUP) * own + known % own
    origin = jnp.where(source >= 0, owner % GROUP, -1)
    half = count // 2
    tile = 128 if half % 128 == 0 else half
    block = (own, height, width)
    wide = (own, line, height, width)
    lane = (line, height, width)
    low = jnp.bfloat16
    return pl.pallas_call(
        functools.partial(kernel, line),
        out_shape=jax.ShapeDtypeStruct((slots, height, width), low),
        in_specs=[pl.BlockSpec(memory_space=pltpu.SMEM)] * 2 + [pl.BlockSpec(memory_space=pl.ANY)] * 4,
        out_specs=pl.BlockSpec(memory_space=pltpu.VMEM),
        scratch_shapes=[
            pltpu.VMEM(block, low),
            pltpu.VMEM((count // tile, tile, field_count), low),
            pltpu.VMEM(fields.shape, jnp.int32),
            pltpu.VMEM((GROUP, 2, half, width), low),
            pltpu.VMEM((GROUP, 2, line * own, half), jnp.float32),
            pltpu.VMEM((GROUP, 2, line * own, half), jnp.float32),
            [pltpu.VMEM(lane, low)] * own,
            pltpu.VMEM(wide, jnp.float32),
            [pltpu.VMEM(lane, low)] * own,
            [pltpu.VMEM(lane, low)] * own,
            pltpu.VMEM(block, jnp.float32),
            [pltpu.VMEM(block[1:], low)] * own,
            [pltpu.VMEM(lane, low)] * own,
            [pltpu.VMEM(lane, low)] * own,
            [pltpu.VMEM(lane, low)] * own,
            [pltpu.VMEM(block[1:], low)] * own,
            [pltpu.VMEM(lane, low)] * own,
            pltpu.VMEM((GROUP, slots, height, width), low),
            pltpu.VMEM((GROUP, slots, height, width), low),
            pltpu.SemaphoreType.DMA((3,)),
            pltpu.SemaphoreType.DMA((count // tile,)),
            pltpu.SemaphoreType.DMA((5, own, line)),
            pltpu.SemaphoreType.DMA((5, own, line)),
            pltpu.SemaphoreType.DMA((2, GROUP)),
            pltpu.SemaphoreType.DMA((2, GROUP)),
            pltpu.SemaphoreType.DMA((5, PIECES)),
            pltpu.SemaphoreType.DMA((5, PIECES)),
        ],
        compiler_params=pltpu.CompilerParams(collective_id=0, has_side_effects=True, vmem_limit_bytes=60000 * 1024),
    )(location, origin, orbitals, points.reshape(2, half, width), coupling, fields)


def solution(mesh):
    return jax.shard_map(
        per_device,
        mesh=mesh,
        in_specs=(
            P(("rep", "pts"), None, None),
            P("pts", None),
            P("pts", None),
            P("rep", None),
            P("rep"),
        ),
        out_specs=P(("rep", "pts"), None, None),
        check_vma=False,
    )
```
